128 devices in a mesh: req: 32 (over y, z, core), kvh: 4 (over x).
Axes of the slice: x: 4, y: 4, z: 4, core: 2. Of those that a mesh axis runs over, the one named last changes fastest.
Arguments:
- queries: bfloat16 [2048, 4, 8, 128], P('req', 'kvh')
- key_cache: bfloat16 [5120, 4, 128, 128], P('req', 'kvh')
- value_cache: bfloat16 [5120, 4, 128, 128], P('req', 'kvh'), may hold values from -24 to 24
- lengths: int32 [2048], P('req'), may hold values from 1 to 4096, as said below
- page_table: int32 [2048, 32], P('req'), may hold values from 0 to 159, as said below
- residual_in: bfloat16 [2048, 2048], P(('req', 'kvh')), may hold values from -4 to 4
- w_out: bfloat16 [4096, 2048], P('kvh'), may hold values from -0.09375 to 0.09375
- norm_gain: bfloat16 [2048], replicated, may hold values from 0.099609375 to 1.8984375
- route_logits: float32 [2048, 8], P(('req', 'kvh'))
- routes: int32 [2048, 8], P(('req', 'kvh')), may hold values from 0 to 127, as said below
- w_gate: bfloat16 [128, 2048, 768], P(('req', 'kvh')), may hold values from -0.125 to 0.125
- w_up: bfloat16 [128, 2048, 768], P(('req', 'kvh')), may hold values from -0.125 to 0.125
- w_down: bfloat16 [128, 768, 2048], P(('req', 'kvh')), may hold values from -0.21875 to 0.21875
Outputs:
- layer_out: bfloat16 [2048, 2048], P(('req', 'kvh'))
The draws below stay inside these ranges and needn't reach their ends.
Inputs may be any that keep to these rules, and one draw needn't show every extreme that they name: `lengths`: every request of a block of 64 has between 1 and 32 pages; some request reaches 4096. `page_table`: local page numbers within the pool of the request's block of 64 requests. Entries 0 to ceil(lengths / 128) - 1 of the requests of one block are all distinct; later entries repeat the request's last used page. `routes`: each token names 8 different experts. Of the 16 tokens of one device, at most 2 name the same expert, and some expert is named by exactly 2 tokens of every device.
All inputs are finite; a program needn't handle non-finite values.
Results may differ from the reference program's by a relative error of at most 0.0054.
Values may be sent and summed in bfloat16 or wider, within the bound.
No kernel may reach another device: no remote copies, remote signals or barrier semaphores. Data moves between devices by JAX's collectives and lax.ppermute only.
A program may use at most 192 MiB of HBM per device.

```python
import jax
import jax.numpy as jnp
from jax import lax

D = 2048
H = 32
KVH = 4
HD = 128
FF = 768
TOP = 8
PAGE = 128
REQ_DEV = 64
G = 8
MAXP = 32
PAGES_DEV = 160
PAGES = 5120
REQUESTS = 2048
TOK_DEV = 16
TOKENS = 2048
EXPERTS = 128
CAP = 2
N_REQ = 32


def cache_layout(key):
    base_key = jax.random.fold_in(key, 101)
    level_key, order_key, tail_key, pool_key = jax.random.split(base_key, 4)
    levels = jax.random.randint(level_key, (N_REQ,), 0, 4).astype(jnp.int32)
    levels = levels.at[0].set(0)
    extra_pages = jnp.right_shift(jnp.full((N_REQ,), PAGES_DEV - REQ_DEV, jnp.int32), levels)
    orders = jax.vmap(lambda block_key: jax.random.permutation(block_key, REQ_DEV))(jax.random.split(order_key, N_REQ))
    rank_in_block = jnp.argsort(orders, axis=1).astype(jnp.int32)
    page_counts = 1 + jnp.clip(extra_pages[:, None] - (MAXP - 1) * rank_in_block, 0, MAXP - 1)
    last_fill = jax.random.randint(tail_key, (N_REQ, REQ_DEV), 1, PAGE + 1).astype(jnp.int32)
    last_fill = jnp.where(page_counts == MAXP, PAGE, last_fill)
    lengths = ((page_counts - 1) * PAGE + last_fill).astype(jnp.int32)
    page_orders = jax.vmap(lambda block_key: jax.random.permutation(block_key, PAGES_DEV))(jax.random.split(pool_key, N_REQ)).astype(jnp.int32)
    offsets = jnp.cumsum(page_counts, axis=1) - page_counts
    columns = jnp.arange(MAXP, dtype=jnp.int32)
    page_spots = offsets[:, :, None] + jnp.minimum(columns[None, None, :], page_counts[:, :, None] - 1)
    page_table = jax.vmap(lambda order_row, spot_rows: order_row[spot_rows])(page_orders, page_spots).astype(jnp.int32)
    return (lengths, page_table)


def key_field_draw(key):
    base_key = jax.random.fold_in(key, 211)
    noise_key, scale_key = jax.random.split(base_key, 2)
    shape = (PAGES, KVH, PAGE, HD)
    values = jax.random.normal(noise_key, shape, jnp.float32)
    spread = jnp.exp(jax.random.uniform(scale_key, (PAGES, KVH, PAGE, 1), jnp.float32, jnp.log(0.3), jnp.log(3.0)))
    key_field = values * spread
    return key_field


def draw_lengths(key, part):
    lengths, page_table = cache_layout(key)
    return lengths.reshape(REQUESTS)


def draw_page_table(key, part):
    lengths, page_table = cache_layout(key)
    return page_table.reshape(REQUESTS, MAXP)


def draw_key_cache(key, part):
    key_field = key_field_draw(key)
    return key_field.astype(jnp.bfloat16)


def draw_queries(key, part):
    base_key = jax.random.fold_in(key, 231)
    noise_key, scale_key = jax.random.split(base_key, 2)
    shape = (REQUESTS, KVH, G, HD)
    values = jax.random.normal(noise_key, shape, jnp.float32)
    spread = jnp.exp(jax.random.uniform(scale_key, (REQUESTS, KVH, G, 1), jnp.float32, jnp.log(0.15), jnp.log(1.5)))
    result = values * spread
    return result.astype(jnp.bfloat16)


def draw_route_logits(key, part):
    base_key = jax.random.fold_in(key, 311)
    noise_key, scale_key = jax.random.split(base_key, 2)
    spread = jnp.exp(jax.random.uniform(scale_key, (TOKENS, 1), jnp.float32, jnp.log(0.4), jnp.log(4.0)))
    values = jax.random.normal(noise_key, (TOKENS, TOP), jnp.float32) * spread
    return values


def draw_routes(key, part):
    base_key = jax.random.fold_in(key, 401)
    weight_key, hot_key, pick_key, shuffle_key = jax.random.split(base_key, 4)
    expert_boost = jnp.left_shift(jnp.ones((EXPERTS,), jnp.int32), jax.random.randint(weight_key, (EXPERTS,), 0, 3).astype(jnp.int32))
    hot_expert = jax.random.randint(hot_key, (), 0, EXPERTS).astype(jnp.int32)
    slot_ids = jnp.arange(EXPERTS * CAP, dtype=jnp.int32)
    slot_owner = slot_ids // CAP

    def block_routes(block_key):
        priority = jax.random.randint(block_key, (EXPERTS * CAP,), 0, 4096).astype(jnp.int32) * expert_boost[slot_owner]
        slot_score = priority * (EXPERTS * CAP) + slot_ids
        slot_score = jnp.where(slot_owner == hot_expert, (1 << 28) + slot_ids, slot_score)
        ignored, chosen = lax.top_k(slot_score, TOK_DEV * TOP)
        ordered = jnp.sort(chosen.astype(jnp.int32)) // CAP
        return ordered.reshape(TOP, TOK_DEV).T
    blocks = TOKENS // TOK_DEV
    picked = jax.vmap(block_routes)(jax.random.split(pick_key, blocks)).reshape(TOKENS, TOP)
    orders = jax.vmap(lambda token_key: jax.random.permutation(token_key, TOP))(jax.random.split(shuffle_key, TOKENS)).astype(jnp.int32)
    return jnp.take_along_axis(picked, orders, axis=1).astype(jnp.int32)


def level_of(rng, shape, cuts, smallest, top_value):
    factor_of, own = 1.0, jax.random.fold_in(rng, 6)
    for dim, parts in cuts:
        heights = jnp.exp(jax.random.uniform(jax.random.fold_in(own, dim), (parts,), jnp.float32, smallest / len(cuts), top_value / len(cuts)))
        factor_of = factor_of * jnp.repeat(heights, shape[dim] // parts).reshape([-1 if axis == dim else 1 for axis in range(len(shape))])
    return factor_of


def gaussian(key, shape, scale, most, shards=(), kind=jnp.bfloat16):
    loudness = level_of(key, shape, shards, -0.22, 0.18) if shards else 1.0
    values = jax.random.normal(key, shape, jnp.float32) * scale * loudness
    return jnp.minimum(jnp.maximum(values, -most), most).astype(kind)


def setup_inputs(seed: int = 0) -> dict:
    arg_keys = jax.random.split(jax.random.key(seed), 14)
    queries = draw_queries(jax.random.fold_in(arg_keys[13], 71), 0)
    key_cache = draw_key_cache(jax.random.fold_in(arg_keys[13], 71), 0)
    value_cache = gaussian(arg_keys[2], (PAGES, KVH, PAGE, HD), 4.0, 24.0, ((0, 32), (1, 4)))
    lengths = draw_lengths(jax.random.fold_in(arg_keys[13], 71), 0)
    page_table = draw_page_table(jax.random.fold_in(arg_keys[13], 71), 0)
    residual_in = gaussian(arg_keys[5], (TOKENS, D), 0.5, 4.0, ((0, 128),))
    w_out = gaussian(arg_keys[6], (H * HD, D), (H * HD) ** -0.5, 0.09375, ((0, 4),))
    norm_gain = jnp.clip(1.0 + 0.18 * jax.random.normal(arg_keys[7], (D,), jnp.float32), 0.099609375, 1.8984375).astype(jnp.bfloat16)
    route_logits = draw_route_logits(jax.random.fold_in(arg_keys[13], 71), 0)
    routes = draw_routes(jax.random.fold_in(arg_keys[13], 71), 0)
    w_gate = gaussian(arg_keys[10], (EXPERTS, D, FF), D ** -0.5, 0.125, ((0, 128),))
    w_up = gaussian(arg_keys[11], (EXPERTS, D, FF), D ** -0.5, 0.125, ((0, 128),))
    w_down = gaussian(arg_keys[12], (EXPERTS, FF, D), FF ** -0.5, 0.21875, ((0, 128),))
    return {"queries": queries, "key_cache": key_cache, "value_cache": value_cache, "lengths": lengths, "page_table": page_table, "residual_in": residual_in, "w_out": w_out, "norm_gain": norm_gain, "route_logits": route_logits, "routes": routes, "w_gate": w_gate, "w_up": w_up, "w_down": w_down}


def swish_gate(gate_part, up_part):
    return gate_part / (1.0 + jnp.exp(-gate_part)) * up_part

def usable_slots(lengths, page_table):
    used_pages = (lengths + PAGE - 1) // PAGE
    columns = jnp.arange(MAXP, dtype=jnp.int32)
    pool_ids = jnp.arange(PAGES_DEV, dtype=jnp.int32)
    matched = (page_table[:, :, None] == pool_ids[None, None, :]) & (columns[None, :, None] < used_pages[:, None, None])
    owned_page = jnp.any(matched, axis=1)
    first_pos = lax.optimization_barrier(jnp.sum(jnp.where(matched, columns[None, :, None] * PAGE, 0), axis=1)).astype(jnp.int32)
    offsets = jnp.arange(PAGE, dtype=jnp.int32)
    position = first_pos[:, :, None] + offsets[None, None, :]
    usable = owned_page[:, :, None] & (position < lengths[:, None, None])
    return usable.reshape(lengths.shape[0], PAGES_DEV * PAGE)

def attend_block(operands):
    queries, key_cache, value_cache, lengths, page_table = operands
    usable = usable_slots(lengths, page_table)
    key_flat = jnp.transpose(key_cache, (1, 0, 2, 3)).reshape(KVH, PAGES_DEV * PAGE, HD).astype(jnp.float32)
    value_flat = jnp.transpose(value_cache, (1, 0, 2, 3)).reshape(KVH, PAGES_DEV * PAGE, HD).astype(jnp.float32)
    scores = jnp.einsum('rhgd,hkd->rhgk', queries.astype(jnp.float32), key_flat) * HD ** (-0.5)
    key_mask = usable[:, None, None, :]
    row_max = lax.optimization_barrier(jnp.max(jnp.where(key_mask, scores, -jnp.inf), axis=-1, keepdims=True))
    weights = jnp.where(key_mask, jnp.exp(scores - row_max), 0.0)
    denominator = lax.optimization_barrier(jnp.sum(weights, axis=-1, keepdims=True))
    rounded = lax.optimization_barrier(weights.astype(jnp.bfloat16))
    mixed_values = jnp.einsum('rhgk,hkd->rhgd', rounded.astype(jnp.float32), value_flat)
    return (mixed_values / denominator).astype(jnp.bfloat16)

def earlier_count(pair_routes):
    positions = jnp.arange(pair_routes.shape[0], dtype=jnp.int32)
    same_expert = pair_routes[:, None] == pair_routes[None, :]
    before = positions[None, :] < positions[:, None]
    return lax.optimization_barrier(jnp.sum(same_expert & before, axis=1)).astype(jnp.int32)

def reference(queries, key_cache, value_cache, lengths, page_table, residual_in, w_out, norm_gain, route_logits, routes, w_gate, w_up, w_down):
    attended = lax.map(attend_block, (queries.reshape(N_REQ, REQ_DEV, KVH, G, HD), key_cache.reshape(N_REQ, PAGES_DEV, KVH, PAGE, HD), value_cache.reshape(N_REQ, PAGES_DEV, KVH, PAGE, HD), lengths.reshape(N_REQ, REQ_DEV), page_table.reshape(N_REQ, REQ_DEV, MAXP)))
    attended = attended.reshape(REQUESTS, KVH * G * HD)
    stream = residual_in.astype(jnp.float32) + jnp.dot(attended, w_out, preferred_element_type=jnp.float32)
    inverse_rms = lax.rsqrt(lax.optimization_barrier(jnp.mean(stream * stream, axis=-1, keepdims=True)) + 1e-06)
    normed = (stream * inverse_rms * norm_gain.astype(jnp.float32)).astype(jnp.bfloat16)
    logit_max = lax.optimization_barrier(jnp.max(route_logits, axis=-1, keepdims=True))
    logit_exp = jnp.exp(route_logits - logit_max)
    gate_weights = logit_exp / lax.optimization_barrier(jnp.sum(logit_exp, axis=-1, keepdims=True))
    device_count = EXPERTS
    pair_routes = routes.reshape(device_count, TOK_DEV * TOP)
    pair_slots = jax.vmap(earlier_count)(pair_routes)
    token_routes = pair_routes.reshape(device_count, TOK_DEV, TOP)
    token_slots = pair_slots.reshape(device_count, TOK_DEV, TOP)
    normed_blocks = normed.reshape(device_count, TOK_DEV, D)
    cap_ids = jnp.arange(CAP, dtype=jnp.int32)

    def run_expert(expert_index):
        picked = jnp.any((token_routes[:, None, :, :] == expert_index) & (token_slots[:, None, :, :] == cap_ids[None, :, None, None]), axis=-1)
        gathered = jnp.einsum('bct,btd->bcd', picked.astype(jnp.float32), normed_blocks.astype(jnp.float32)).astype(jnp.bfloat16)
        flat_rows = gathered.reshape(device_count * CAP, D)
        gate_part = jnp.dot(flat_rows, w_gate[expert_index], preferred_element_type=jnp.float32)
        up_part = jnp.dot(flat_rows, w_up[expert_index], preferred_element_type=jnp.float32)
        hidden = swish_gate(gate_part, up_part).astype(jnp.bfloat16)
        produced = jnp.dot(hidden, w_down[expert_index], preferred_element_type=jnp.float32).astype(jnp.bfloat16)
        return produced.reshape(device_count, CAP, D)
    outputs = lax.map(run_expert, jnp.arange(EXPERTS, dtype=jnp.int32))
    block_ids = jnp.broadcast_to(jnp.arange(device_count, dtype=jnp.int32)[:, None], pair_routes.shape)
    fetched = outputs[pair_routes, block_ids, pair_slots].astype(jnp.float32).reshape(TOKENS, TOP, D)
    mixture = lax.optimization_barrier(jnp.sum(gate_weights[:, :, None] * fetched, axis=1))
    return (stream + mixture).astype(jnp.bfloat16)
```

```python
import functools

import jax
import jax.numpy as jnp
from jax import lax
from jax.experimental import pallas as pl
from jax.experimental.pallas import tpu as pltpu
from jax.sharding import PartitionSpec as P

AXES = ("req", "kvh")
BLOCK = 32
COLS = 4
FOLD = 4


def dot32(a, b):
    return jnp.dot(a, b, preferred_element_type=jnp.float32)


def stay(x):
    return pltpu.with_memory_space_constraint(x, pltpu.HBM)


def iota(shape, axis):
    return lax.broadcasted_iota(jnp.int32, shape, axis)


def attend_kernel(
    len_hbm, table_hbm, q_hbm, k_hbm, v_hbm, w_hbm, out_hbm,
    len_ref, table_ref, q_ref, k_buf, v_buf, w_buf, owner, left, m_ref, l_ref, o_ref, att_ref, out_buf,
    in_sem, k_sem, v_sem, out_sem,
):
    pages, slots, dim = k_buf.shape
    requests, groups, _ = q_ref.shape
    blocks = pages // BLOCK
    table_copies = (
        pltpu.make_async_copy(len_hbm, len_ref, in_sem.at[0]),
        pltpu.make_async_copy(table_hbm, table_ref, in_sem.at[1]),
    )
    q_copy = pltpu.make_async_copy(q_hbm, q_ref, in_sem.at[2])
    w_copy = pltpu.make_async_copy(w_hbm, w_buf, in_sem.at[3])
    for copy in table_copies:
        copy.start()
    q_copy.start()

    def copies(b):
        span = pl.ds(b * BLOCK, BLOCK)
        return (
            pltpu.make_async_copy(k_hbm.at[span], k_buf.at[span], k_sem.at[b]),
            pltpu.make_async_copy(v_hbm.at[span], v_buf.at[span], v_sem.at[b]),
        )

    for b in range(blocks):
        for copy in copies(b):
            copy.start()
    w_copy.start()
    m_ref[...] = jnp.full(m_ref.shape, -jnp.inf, jnp.float32)
    l_ref[...] = jnp.zeros(l_ref.shape, jnp.float32)
    o_ref[...] = jnp.zeros(o_ref.shape, jnp.float32)
    for copy in table_copies:
        copy.wait()

    @pl.loop(0, pages, unroll=8)
    def _(p):
        owner[p] = requests
        left[p] = 0

    @pl.loop(0, requests)
    def _(r):
        length = len_ref[r]

        @pl.loop(0, (length + slots - 1) >> (slots.bit_length() - 1))
        def _(j):
            p = table_ref[j, r]
            owner[p] = r
            left[p] = length - j * slots

    q_copy.wait()
    lane = iota((groups, slots), 1)

    @pl.loop(0, blocks)
    def _(b):
        for copy in copies(b):
            copy.wait()
        ids = [b * BLOCK + i for i in range(BLOCK)]
        own = [owner[p] for p in ids]
        scores, peaks = [], []
        for p, r in zip(ids, own):
            q = q_ref[jnp.minimum(r, requests - 1)]
            s = lax.dot_general(
                q, k_buf[p], (((1,), (1,)), ((), ())), preferred_element_type=jnp.float32
            ) * dim ** (-0.5)
            s = jnp.where(lane < left[p], s, -jnp.inf)
            scores.append(s)
            peaks.append(jnp.max(s, axis=-1, keepdims=True))
        shrink, weights = [], []
        for s, peak, r in zip(scores, peaks, own):
            old = m_ref[r]
            new = jnp.maximum(old, peak)
            m_ref[r] = new
            shrink.append(jnp.exp(old - new))
            weights.append(jnp.exp(s - new))
        for a, w, r, p in zip(shrink, weights, own, ids):
            mixed = dot32(w.astype(jnp.bfloat16), v_buf[p])
            l_ref[r] = a * l_ref[r] + w
            o_ref[r] = a * o_ref[r] + mixed

    for g in range(groups):
        total = jnp.sum(l_ref[:requests, g, :], axis=-1, keepdims=True)
        att_ref[:, g * dim:(g + 1) * dim] = (o_ref[:requests, g, :] / total).astype(jnp.bfloat16)
    w_copy.wait()
    att = att_ref[...]
    cols = out_buf.shape[1] // COLS
    writes = []
    for c in range(COLS):
        span = slice(c * cols, (c + 1) * cols)
        out_buf[:, span] = dot32(att, w_buf[:, span]).astype(out_buf.dtype)
        write = pltpu.make_async_copy(out_buf.at[:, span], out_hbm.at[:, span], out_sem.at[c])
        write.start()
        writes.append(write)
    for write in writes:
        write.wait()


def attend(lengths, page_table, queries, key_cache, value_cache, w_out):
    pages, slots, dim = key_cache.shape
    requests, groups, _ = queries.shape
    blocks = pages // BLOCK
    hbm = pl.BlockSpec(memory_space=pltpu.HBM)
    rows = (requests + 1, groups, dim)
    return pl.pallas_call(
        attend_kernel,
        out_shape=pltpu.HBM((requests, w_out.shape[1]), jnp.bfloat16),
        in_specs=[hbm] * 6,
        out_specs=hbm,
        scratch_shapes=[
            pltpu.SMEM(lengths.shape, jnp.int32),
            pltpu.SMEM(page_table.shape, jnp.int32),
            pltpu.VMEM(queries.shape, queries.dtype),
            pltpu.VMEM(key_cache.shape, key_cache.dtype),
            pltpu.VMEM(value_cache.shape, value_cache.dtype),
            pltpu.VMEM(w_out.shape, w_out.dtype),
            pltpu.SMEM((pages,), jnp.int32),
            pltpu.SMEM((pages,), jnp.int32),
            pltpu.VMEM(rows, jnp.float32),
            pltpu.VMEM(rows, jnp.float32),
            pltpu.VMEM(rows, jnp.float32),
            pltpu.VMEM((requests, groups * dim), jnp.bfloat16),
            pltpu.VMEM((requests, w_out.shape[1]), jnp.bfloat16),
            pltpu.SemaphoreType.DMA((4,)),
            pltpu.SemaphoreType.DMA((blocks,)),
            pltpu.SemaphoreType.DMA((blocks,)),
            pltpu.SemaphoreType.DMA((COLS,)),
        ],
        compiler_params=pltpu.CompilerParams(vmem_limit_bytes=24 << 20),
        name="attend",
    )(*map(stay, (lengths, page_table, queries, key_cache, value_cache, w_out)))


def plan_kernel(routes_t_ref, routes_ref, logits_ref, res_ref, send_ref, high_ref, low_ref, stay_ref):
    picks, tokens = routes_t_ref.shape
    rows, lanes = send_ref.shape
    stay_ref[...] = res_ref[...]
    src, dst = iota((lanes, lanes), 0), iota((lanes, lanes), 1)
    alike = (src & -tokens) == (dst & -tokens)
    before = ((src < dst) & alike).astype(jnp.float32).astype(jnp.bfloat16)
    after = ((src > dst) & alike).astype(jnp.float32).astype(jnp.bfloat16)

    spread = iota((tokens, lanes), 0) == (iota((tokens, lanes), 1) & (tokens - 1))
    named = dot32(
        routes_t_ref[...].astype(jnp.float32).astype(jnp.bfloat16),
        spread.astype(jnp.float32).astype(jnp.bfloat16),
    ).astype(jnp.int32)
    step = 256
    for start in range(0, rows, step):
        row = iota((step, lanes), 0) + start
        col = iota((step, lanes), 1)
        target = row >> 3
        has = named[0:1, :] == target
        for k in range(1, picks):
            has = has | (named[k:k + 1, :] == target)
        count = dot32(has.astype(jnp.float32).astype(jnp.bfloat16), before)
        fits = (count == (row & 1).astype(jnp.float32)) & (((row >> 1) & (FOLD - 1)) == col // tokens)
        send_ref[start:start + step, :] = (has & fits).astype(jnp.float32).astype(jnp.bfloat16)

    logits = logits_ref[...]
    raised = jnp.exp(logits - jnp.max(logits, axis=-1, keepdims=True))
    gates = raised / jnp.sum(raised, axis=-1, keepdims=True)
    gates = jnp.concatenate([gates] * FOLD, axis=0)
    routes = jnp.concatenate([routes_ref[...]] * FOLD, axis=0)
    for start in range(0, rows, step):
        col = iota((lanes, step), 1) + start
        row = iota((lanes, step), 0)
        target = col >> 3
        mix = jnp.zeros((lanes, step), jnp.float32)
        has = jnp.zeros((lanes, step), jnp.float32)
        for k in range(picks):
            same = routes[:, k:k + 1] == target
            mix = jnp.where(same, gates[:, k:k + 1], mix)
            has = jnp.where(same, 1.0, has)
        count = dot32(after, has.astype(jnp.bfloat16))
        fits = (count == (col & 1).astype(jnp.float32)) & (((col >> 1) & (FOLD - 1)) == row // tokens)
        mix = jnp.where(fits, mix, 0.0)
        high = mix.astype(jnp.bfloat16)
        high_ref[:, start:start + step] = high
        low_ref[:, start:start + step] = (mix - high.astype(jnp.float32)).astype(jnp.bfloat16)


def plan(routes, route_logits, residual, experts):
    tokens = routes.shape[0]
    rows, lanes = experts * 2 * FOLD, FOLD * tokens
    vmem = pl.BlockSpec(memory_space=pltpu.VMEM)
    return pl.pallas_call(
        plan_kernel,
        out_shape=(
            jax.ShapeDtypeStruct((rows, lanes), jnp.bfloat16),
            jax.ShapeDtypeStruct((lanes, rows), jnp.bfloat16),
            jax.ShapeDtypeStruct((lanes, rows), jnp.bfloat16),
            jax.ShapeDtypeStruct(residual.shape, residual.dtype),
        ),
        in_specs=[vmem] * 4,
        out_specs=(vmem,) * 4,
        compiler_params=pltpu.CompilerParams(vmem_limit_bytes=8 << 20),
        name="plan",
    )(routes.T, routes, route_logits, residual)


def dispatch_kernel(part_ref, res_ref, gain_ref, send_ref, stream_ref, out_ref):
    width = res_ref.shape[1]
    part = width // FOLD
    total = part_ref[0].astype(jnp.float32)
    for i in range(1, part_ref.shape[0]):
        total = total + part_ref[i].astype(jnp.float32)
    stream = res_ref[...].astype(jnp.float32) + total
    stream_ref[...] = stream
    inverse = lax.rsqrt(jnp.mean(stream * stream, axis=-1, keepdims=True) + 1e-06)
    normed = (stream * inverse * gain_ref[...].astype(jnp.float32)).astype(jnp.bfloat16)
    rows = jnp.concatenate([normed[:, f * part:(f + 1) * part] for f in range(FOLD)], axis=0)
    out_ref[...] = dot32(send_ref[...], rows).astype(out_ref.dtype)


def dispatch(parts, residual, gain, send):
    tokens, width = residual.shape
    vmem = pl.BlockSpec(memory_space=pltpu.VMEM)
    return pl.pallas_call(
        dispatch_kernel,
        out_shape=(
            jax.ShapeDtypeStruct((tokens, width), jnp.float32),
            jax.ShapeDtypeStruct((send.shape[0], width // FOLD), jnp.bfloat16),
        ),
        in_specs=[vmem] * 4,
        out_specs=(vmem, vmem),
        compiler_params=pltpu.CompilerParams(vmem_limit_bytes=8 << 20),
        name="dispatch",
    )(parts, residual, gain, send)


def expert_kernel(x_ref, gate_ref, up_hbm, down_hbm, out_ref, x_buf, up_ref, down_ref, sem):
    rows, part = x_ref.shape
    up_copy = pltpu.make_async_copy(up_hbm, up_ref, sem.at[0])
    down_copy = pltpu.make_async_copy(down_hbm, down_ref, sem.at[1])
    up_copy.start()
    down_copy.start()
    group = 128
    inner = group // FOLD
    j, i = iota((group, group), 0), iota((group, group), 1)

    def source(row):
        return ((row & (inner - 1)) >> 1) * (2 * FOLD) + (row // inner) * 2 + (row & 1)

    unfold = (i == source(j)).astype(jnp.float32).astype(jnp.bfloat16)
    refold = (j == source(i)).astype(jnp.float32).astype(jnp.bfloat16)
    for n in range(rows // group):
        piece = dot32(unfold, x_ref[n * group:(n + 1) * group, :]).astype(jnp.bfloat16)
        for f in range(FOLD):
            x_buf[n * inner:(n + 1) * inner, f * part:(f + 1) * part] = piece[f * inner:(f + 1) * inner]
    x = x_buf[...]
    gate = dot32(x, gate_ref[...])
    up_copy.wait()
    up = dot32(x, up_ref[...])
    hidden = (gate / (1.0 + jnp.exp(-gate)) * up).astype(jnp.bfloat16)
    down_copy.wait()
    made = dot32(hidden, down_ref[...]).astype(jnp.bfloat16)
    for n in range(rows // group):
        piece = jnp.concatenate(
            [made[n * inner:(n + 1) * inner, f * part:(f + 1) * part] for f in range(FOLD)], axis=0
        )
        out_ref[n * group:(n + 1) * group, :] = dot32(refold, piece).astype(out_ref.dtype)


def expert(arrived, w_gate, w_up, w_down):
    vmem = pl.BlockSpec(memory_space=pltpu.VMEM)
    hbm = pl.BlockSpec(memory_space=pltpu.HBM)
    rows, part = arrived.shape
    return pl.pallas_call(
        expert_kernel,
        out_shape=jax.ShapeDtypeStruct(arrived.shape, jnp.bfloat16),
        in_specs=[vmem, vmem, hbm, hbm],
        out_specs=vmem,
        scratch_shapes=[
            pltpu.VMEM((rows // FOLD, part * FOLD), jnp.bfloat16),
            pltpu.VMEM(w_up.shape, w_up.dtype),
            pltpu.VMEM(w_down.shape, w_down.dtype),
            pltpu.SemaphoreType.DMA((2,)),
        ],
        compiler_params=pltpu.CompilerParams(vmem_limit_bytes=32 << 20),
        name="expert",
    )(arrived, w_gate, stay(w_up), stay(w_down))


def combine_kernel(back_ref, stream_ref, high_ref, low_ref, out_ref):
    tokens = stream_ref.shape[0]
    part = back_ref.shape[1]
    back = back_ref[...]
    total = dot32(high_ref[...], back) + dot32(low_ref[...], back)
    for f in range(FOLD):
        span = slice(f * part, (f + 1) * part)
        out_ref[:, span] = (stream_ref[:, span] + total[f * tokens:(f + 1) * tokens]).astype(out_ref.dtype)


def combine(back, stream, high, low):
    vmem = pl.BlockSpec(memory_space=pltpu.VMEM)
    return pl.pallas_call(
        combine_kernel,
        out_shape=jax.ShapeDtypeStruct(stream.shape, jnp.bfloat16),
        in_specs=[vmem] * 4,
        out_specs=vmem,
        compiler_params=pltpu.CompilerParams(vmem_limit_bytes=8 << 20),
        name="combine",
    )(back, stream, high, low)


def local(
    queries,
    key_cache,
    value_cache,
    lengths,
    page_table,
    residual_in,
    w_out,
    norm_gain,
    route_logits,
    routes,
    w_gate,
    w_up,
    w_down,
):
    heads = lax.axis_size("kvh")
    experts = lax.axis_size("req") * heads
    partial = attend(lengths, page_table.T, queries[:, 0], key_cache[:, 0], value_cache[:, 0], w_out)
    tokens, width = residual_in.shape
    parts = lax.all_to_all(
        partial.reshape(heads, tokens, width), "kvh", split_axis=0, concat_axis=0, tiled=True
    )
    send, high, low, residual = plan(routes, route_logits, residual_in, experts)
    stream, outgoing = dispatch(parts, residual, norm_gain[None, :], send)
    layout = (experts, 2 * FOLD, width // FOLD)
    exchange = functools.partial(lax.all_to_all, axis_name=AXES, split_axis=0, concat_axis=0, tiled=True)
    arrived = exchange(outgoing.reshape(layout)).reshape(outgoing.shape)
    produced = expert(arrived, w_gate[0], w_up[0], w_down[0])
    back = exchange(produced.reshape(layout)).reshape(outgoing.shape)
    return combine(back, stream, high, low)


def solution(mesh):
    in_specs = (
        P("req", "kvh", None, None),
        P("req", "kvh", None, None),
        P("req", "kvh", None, None),
        P("req"),
        P("req", None),
        P(AXES, None),
        P("kvh", None),
        P(),
        P(AXES, None),
        P(AXES, None),
        P(AXES, None, None),
        P(AXES, None, None),
        P(AXES, None, None),
    )
    return jax.shard_map(
        local, mesh=mesh, in_specs=in_specs, out_specs=P(AXES, None), check_vma=False
    )
```

```python
import functools

import jax
import jax.numpy as jnp
from jax import lax
from jax.experimental import pallas as pl
from jax.experimental.pallas import tpu as pltpu
from jax.sharding import PartitionSpec as P

AXES = ("req", "kvh")
BLOCK = 80
COLS = 4
FOLD = 4


def dot32(a, b):
    return jnp.dot(a, b, preferred_element_type=jnp.float32)


def stay(x):
    return pltpu.with_memory_space_constraint(x, pltpu.HBM)


def dot_t(a, b):
    return lax.dot_general(a, b, (((1,), (1,)), ((), ())), preferred_element_type=jnp.float32)


def flags(mask):
    return mask.astype(jnp.float32).astype(jnp.bfloat16)


def iota(shape, axis):
    return lax.broadcasted_iota(jnp.int32, shape, axis)


def plan(routes, gates, send_ref, mix_ref):
    picks, tokens = routes.shape
    rows, lanes = send_ref.shape
    experts = rows // (2 * FOLD)
    spread = flags(iota((lanes, tokens), 1) == (iota((lanes, tokens), 0) & (tokens - 1)))
    high = gates.astype(jnp.bfloat16)
    low = (gates - high.astype(jnp.float32)).astype(jnp.bfloat16)
    named = dot_t(spread, routes.astype(jnp.float32).astype(jnp.bfloat16))
    highs, lows = dot_t(spread, high), dot_t(spread, low)
    expert = iota((lanes, experts), 1).astype(jnp.float32)
    has = jnp.zeros((lanes, experts), jnp.float32)
    mix_high, mix_low = has, has
    for k in range(picks):
        match = named[:, k:k + 1] == expert
        has = jnp.where(match, 1.0, has)
        mix_high = jnp.where(match, highs[:, k:k + 1], mix_high)
        mix_low = jnp.where(match, lows[:, k:k + 1], mix_low)
    dst, src = iota((lanes, lanes), 0), iota((lanes, lanes), 1)
    before = flags((src < dst) & ((src & -tokens) == (dst & -tokens)))
    count = dot32(before, has.astype(jnp.bfloat16))

    pieces = 4
    span, step = experts // pieces, rows // pieces
    row, col = iota((step, 2 * span), 0), iota((step, 2 * span), 1)
    place = flags(((row & 1) * span + (row >> 3)) == col)
    keep = ((iota((step, lanes), 0) >> 1) & (FOLD - 1)) == iota((step, lanes), 1) // tokens
    row, col = iota((2 * span, step), 0), iota((2 * span, step), 1)
    place_t = flags(((col & 1) * span + (col >> 3)) == row)
    keep_t = ((iota((2 * lanes, step), 1) >> 1) & (FOLD - 1)) == (iota((2 * lanes, step), 0) & (lanes - 1)) // tokens

    def by_slot(values, n):
        part = slice(n * span, (n + 1) * span)
        return jnp.concatenate(
            [jnp.where(count[:, part] == float(c), values[:, part], 0.0) for c in range(2)], axis=1
        ).astype(jnp.bfloat16)

    for n in range(pieces):
        out = slice(n * step, (n + 1) * step)
        sends = dot_t(place, by_slot(has, n))
        send_ref[out, :] = jnp.where(keep, sends, 0.0).astype(jnp.bfloat16)
        mixes = jnp.concatenate([by_slot(mix_high, n), by_slot(mix_low, n)], axis=0)
        mix_ref[:, out] = jnp.where(keep_t, dot32(mixes, place_t), 0.0).astype(jnp.bfloat16)


def attend_kernel(
    len_hbm, table_hbm, q_hbm, k_hbm, v_hbm, w_hbm, routes_hbm, logits_hbm, res_hbm, gain_hbm,
    out_ref, send_ref, mix_ref, res_ref, gain_ref,
    len_ref, table_ref, q_ref, k_buf, v_buf, w_buf, routes_ref, logits_ref,
    apart_ref, left_ref, s_ref, m_ref, o_ref, att_ref,
    in_sem, k_sem, v_sem, w_sem,
):
    pages, slots, dim = k_buf.shape
    requests, groups, _ = q_ref.shape
    columns = table_ref.shape[0]
    blocks = pages // BLOCK
    cols = out_ref.shape[1] // COLS

    def fetch(n, src, dst):
        return pltpu.make_async_copy(src, dst, in_sem.at[n])

    small = [
        fetch(0, len_hbm, len_ref), fetch(1, table_hbm, table_ref), fetch(2, q_hbm, q_ref),
        fetch(3, routes_hbm, routes_ref), fetch(4, logits_hbm, logits_ref),
        fetch(5, res_hbm, res_ref), fetch(6, gain_hbm, gain_ref),
    ]
    k_copies, v_copies = [], []
    for b in range(blocks):
        span = pl.ds(b * BLOCK, BLOCK)
        k_copies.append(pltpu.make_async_copy(k_hbm.at[span], k_buf.at[span], k_sem.at[b]))
        v_copies.append(pltpu.make_async_copy(v_hbm.at[span], v_buf.at[span], v_sem.at[b]))
    w_copies = []
    for c in range(COLS):
        span = slice(c * cols, (c + 1) * cols)
        w_copies.append(pltpu.make_async_copy(w_hbm.at[:, span], w_buf.at[:, span], w_sem.at[c]))
    for copy in small[:3] + k_copies + small[3:] + v_copies + w_copies:
        copy.start()

    small[0].wait()
    small[1].wait()
    lengths = len_ref[...]
    column = iota((columns, requests), 0)
    table = jnp.where(column < ((lengths + (slots - 1)) >> (slots.bit_length() - 1)), table_ref[...], -1)
    usable = lengths - column * slots
    half = columns // 2
    table = jnp.concatenate([table[:half], table[half:]], axis=1)
    usable = jnp.concatenate([usable[:half], usable[half:]], axis=1)
    page = iota((pages, 2 * requests), 0)
    left = jnp.zeros((pages, 2 * requests), jnp.int32)
    for c in range(half):
        left = jnp.where(table[c:c + 1, :] == page, usable[c:c + 1, :], left)
    left = left.astype(jnp.float32)
    owned = jnp.maximum(left[:, :requests], left[:, requests:]) > 0
    left_ref[...] = jnp.broadcast_to(jnp.max(left, axis=-1, keepdims=True), left_ref.shape)
    apart_ref[...] = jnp.where(owned, 0.0, -jnp.inf)
    owned = flags(owned)
    same = flags(iota((requests, requests), 0) == iota((requests, requests), 1))
    pick = dot_t(same, owned).astype(jnp.bfloat16)

    def pair_rows(p):
        return pl.ds(p * groups, 2 * groups)

    def apart_rows(x):
        top = iota(x.shape, 0) < groups
        return jnp.concatenate([jnp.where(top, x, 0.0), jnp.where(top, 0.0, x)], axis=1).astype(jnp.bfloat16)

    def group_rows(g, count):
        return pl.ds(g, count, stride=groups)

    small[2].wait()
    o_ref[:requests * groups, :] = q_ref[...].reshape(requests * groups, dim).astype(jnp.float32)
    for g in range(groups):
        s_ref[group_rows(g, pages), :] = dot32(owned, o_ref[group_rows(g, requests), :].astype(jnp.bfloat16))

    lane = iota((2 * groups, slots), 1).astype(jnp.float32)
    for b in range(blocks):
        k_copies[b].wait()

        for p in range(b * BLOCK, (b + 1) * BLOCK, 2):
            keys = jnp.concatenate([k_buf[p], k_buf[p + 1]], axis=1)
            s = dot_t(apart_rows(s_ref[pair_rows(p), :]), keys) * dim ** (-0.5)
            limit = jnp.concatenate(
                [left_ref[pl.ds(p + i, groups, stride=0), :] for i in range(2)], axis=0
            )
            s = jnp.where(lane < limit, s, -jnp.inf)
            s_ref[pair_rows(p), :] = s
            m_ref[pair_rows(p), :] = jnp.broadcast_to(jnp.max(s, axis=-1, keepdims=True), s.shape)

    apart = apart_ref[...]
    for g in range(groups):
        peak = jnp.max(m_ref[group_rows(g, pages), :][:, :requests] + apart, axis=0, keepdims=True)
        peak = jnp.maximum(jnp.max(peak + apart, axis=-1, keepdims=True), -3e38)
        m_ref[group_rows(g, pages), :] = jnp.broadcast_to(peak, (pages, dim))

    for copy in small[3:]:
        copy.wait()
    logits = logits_ref[...]
    raised = jnp.exp(logits - jnp.max(logits, axis=0, keepdims=True))
    plan(
        routes_ref[...], raised / jnp.sum(raised, axis=0, keepdims=True), send_ref, mix_ref
    )

    for b in range(blocks):
        v_copies[b].wait()

        for p in range(b * BLOCK, (b + 1) * BLOCK, 2):
            w = jnp.exp(s_ref[pair_rows(p), :] - m_ref[pair_rows(p), :])
            m_ref[pair_rows(p), :] = jnp.broadcast_to(jnp.sum(w, axis=-1, keepdims=True), w.shape)
            values = jnp.concatenate([v_buf[p], v_buf[p + 1]], axis=0)
            o_ref[pair_rows(p), :] = dot32(apart_rows(w), values)

    def parts(values):
        high = values.astype(jnp.bfloat16).astype(jnp.float32)
        return high, values - high

    first = iota((pages, dim), 1) < dim // 2
    for g in range(groups):
        high, low = parts(o_ref[group_rows(g, pages), :])
        sums = jnp.where(first, *parts(m_ref[group_rows(g, pages), :]))
        total = dot32(pick, jnp.concatenate([high, low, sums], axis=1).astype(jnp.bfloat16))
        weight = total[:, 2 * dim:]
        weight = weight + pltpu.roll(weight, dim // 2, 1)
        att_ref[:, g * dim:(g + 1) * dim] = (
            (total[:, :dim] + total[:, dim:2 * dim]) / weight
        ).astype(jnp.bfloat16)

    att = att_ref[...]
    for c in range(COLS):
        span = slice(c * cols, (c + 1) * cols)
        w_copies[c].wait()
        out_ref[:, span] = dot32(att, w_buf[:, span]).astype(out_ref.dtype)


def attend(lengths, page_table, queries, key_cache, value_cache, w_out, routes, logits, residual, gain, experts):
    pages, slots, dim = key_cache.shape
    requests, groups, _ = queries.shape
    tokens = residual.shape[0]
    blocks = pages // BLOCK
    hbm = pl.BlockSpec(memory_space=pltpu.HBM)
    vmem = pl.BlockSpec(memory_space=pltpu.VMEM)
    rows, lanes = experts * 2 * FOLD, FOLD * tokens
    tile = pltpu.VMEM((pages * groups, dim), jnp.float32)
    args = (lengths, page_table, queries, key_cache, value_cache, w_out, routes, logits, residual, gain)
    return pl.pallas_call(
        attend_kernel,
        out_shape=(
            jax.ShapeDtypeStruct((requests, w_out.shape[1]), jnp.bfloat16),
            jax.ShapeDtypeStruct((rows, lanes), jnp.bfloat16),
            jax.ShapeDtypeStruct((2 * lanes, rows), jnp.bfloat16),
            jax.ShapeDtypeStruct(residual.shape, residual.dtype),
            jax.ShapeDtypeStruct(gain.shape, gain.dtype),
        ),
        in_specs=[hbm] * len(args),
        out_specs=(vmem,) * 5,
        scratch_shapes=[
            pltpu.VMEM(lengths.shape, jnp.int32),
            pltpu.VMEM(page_table.shape, jnp.int32),
            pltpu.VMEM(queries.shape, queries.dtype),
            pltpu.VMEM(key_cache.shape, key_cache.dtype),
            pltpu.VMEM(value_cache.shape, value_cache.dtype),
            pltpu.VMEM(w_out.shape, w_out.dtype),
            pltpu.VMEM(routes.shape, jnp.int32),
            pltpu.VMEM(logits.shape, jnp.float32),
            pltpu.VMEM((pages, requests), jnp.float32),
            pltpu.VMEM((pages, slots), jnp.float32),
            tile, tile, tile,
            pltpu.VMEM((requests, groups * dim), jnp.bfloat16),
            pltpu.SemaphoreType.DMA((7,)),
            pltpu.SemaphoreType.DMA((blocks,)),
            pltpu.SemaphoreType.DMA((blocks,)),
            pltpu.SemaphoreType.DMA((COLS,)),
        ],
        compiler_params=pltpu.CompilerParams(vmem_limit_bytes=24 << 20),
        name="attend",
    )(*map(stay, args))


def dispatch_kernel(part_ref, res_ref, gain_ref, send_ref, stream_ref, out_ref):
    width = res_ref.shape[1]
    part = width // FOLD
    total = part_ref[0].astype(jnp.float32)
    for i in range(1, part_ref.shape[0]):
        total = total + part_ref[i].astype(jnp.float32)
    stream = res_ref[...].astype(jnp.float32) + total
    stream_ref[...] = stream
    inverse = lax.rsqrt(jnp.mean(stream * stream, axis=-1, keepdims=True) + 1e-06)
    gain = gain_ref[...].astype(jnp.float32)
    gain = jnp.concatenate([gain[i:i + 1] for i in range(gain.shape[0])], axis=1)
    normed = (stream * inverse * gain).astype(jnp.bfloat16)
    rows = jnp.concatenate([normed[:, f * part:(f + 1) * part] for f in range(FOLD)], axis=0)
    out_ref[...] = dot32(send_ref[...], rows).astype(out_ref.dtype)


def dispatch(parts, residual, gain, send):
    tokens, width = residual.shape
    vmem = pl.BlockSpec(memory_space=pltpu.VMEM)
    return pl.pallas_call(
        dispatch_kernel,
        out_shape=(
            jax.ShapeDtypeStruct((tokens, width), jnp.float32),
            jax.ShapeDtypeStruct((send.shape[0], width // FOLD), jnp.bfloat16),
        ),
        in_specs=[vmem] * 4,
        out_specs=(vmem, vmem),
        compiler_params=pltpu.CompilerParams(vmem_limit_bytes=8 << 20),
        name="dispatch",
    )(parts, residual, gain, send)


def expert_kernel(x_ref, gate_ref, up_ref, down_ref, out_ref, x_buf):
    rows, part = x_ref.shape
    group = 128
    inner = group // FOLD
    j, i = iota((group, group), 0), iota((group, group), 1)

    def source(row):
        return ((row & (inner - 1)) >> 1) * (2 * FOLD) + (row // inner) * 2 + (row & 1)

    unfold = (i == source(j)).astype(jnp.float32).astype(jnp.bfloat16)
    refold = (j == source(i)).astype(jnp.float32).astype(jnp.bfloat16)
    for n in range(rows // group):
        piece = dot32(unfold, x_ref[n * group:(n + 1) * group, :]).astype(jnp.bfloat16)
        for f in range(FOLD):
            x_buf[n * inner:(n + 1) * inner, f * part:(f + 1) * part] = piece[f * inner:(f + 1) * inner]
    x = x_buf[...]
    gate = dot32(x, gate_ref[...])
    up = dot32(x, up_ref[...])
    hidden = (gate / (1.0 + jnp.exp(-gate)) * up).astype(jnp.bfloat16)
    made = dot32(hidden, down_ref[...]).astype(jnp.bfloat16)
    for n in range(rows // group):
        piece = jnp.concatenate(
            [made[n * inner:(n + 1) * inner, f * part:(f + 1) * part] for f in range(FOLD)], axis=0
        )
        out_ref[n * group:(n + 1) * group, :] = dot32(refold, piece).astype(out_ref.dtype)


def expert(arrived, w_gate, w_up, w_down):
    vmem = pl.BlockSpec(memory_space=pltpu.VMEM)
    hbm = pl.BlockSpec(memory_space=pltpu.HBM)
    rows, part = arrived.shape
    return pl.pallas_call(
        expert_kernel,
        out_shape=jax.ShapeDtypeStruct(arrived.shape, jnp.bfloat16),
        in_specs=[vmem] * 4,
        out_specs=vmem,
        scratch_shapes=[
            pltpu.VMEM((rows // FOLD, part * FOLD), jnp.bfloat16),
        ],
        compiler_params=pltpu.CompilerParams(vmem_limit_bytes=16 << 20),
        name="expert",
    )(arrived, w_gate, w_up, w_down)


def combine_kernel(back_ref, stream_ref, mix_ref, out_ref):
    tokens = stream_ref.shape[0]
    part = back_ref.shape[1]
    total = dot32(mix_ref[...], back_ref[...])
    total = total[:FOLD * tokens] + total[FOLD * tokens:]
    for f in range(FOLD):
        span = slice(f * part, (f + 1) * part)
        out_ref[:, span] = (stream_ref[:, span] + total[f * tokens:(f + 1) * tokens]).astype(out_ref.dtype)


def combine(back, stream, mix):
    vmem = pl.BlockSpec(memory_space=pltpu.VMEM)
    return pl.pallas_call(
        combine_kernel,
        out_shape=jax.ShapeDtypeStruct(stream.shape, jnp.bfloat16),
        in_specs=[vmem] * 3,
        out_specs=vmem,
        compiler_params=pltpu.CompilerParams(vmem_limit_bytes=8 << 20),
        name="combine",
    )(back, stream, mix)


def local(
    queries,
    key_cache,
    value_cache,
    lengths,
    page_table,
    residual_in,
    w_out,
    norm_gain,
    route_logits,
    routes,
    w_gate,
    w_up,
    w_down,
):
    heads = lax.axis_size("kvh")
    experts = lax.axis_size("req") * heads
    tokens, width = residual_in.shape
    partial, send, mix, residual, gain = attend(
        lengths[None, :], page_table.T, queries[:, 0], key_cache[:, 0], value_cache[:, 0], w_out,
        routes.T, route_logits.T, residual_in, norm_gain.reshape(-1, 128), experts,
    )
    parts = lax.all_to_all(
        partial.reshape(heads, tokens, width), "kvh", split_axis=0, concat_axis=0, tiled=True
    )
    stream, outgoing = dispatch(parts, residual, gain, send)
    layout = (experts, 2 * FOLD, width // FOLD)
    exchange = functools.partial(lax.all_to_all, axis_name=AXES, split_axis=0, concat_axis=0, tiled=True)
    arrived = exchange(outgoing.reshape(layout)).reshape(outgoing.shape)
    produced = expert(arrived, w_gate[0], w_up[0], w_down[0])
    back = exchange(produced.reshape(layout)).reshape(outgoing.shape)
    return combine(back, stream, mix)


def solution(mesh):
    in_specs = (
        P("req", "kvh", None, None),
        P("req", "kvh", None, None),
        P("req", "kvh", None, None),
        P("req"),
        P("req", None),
        P(AXES, None),
        P("kvh", None),
        P(),
        P(AXES, None),
        P(AXES, None),
        P(AXES, None, None),
        P(AXES, None, None),
        P(AXES, None, None),
    )
    return jax.shard_map(
        local, mesh=mesh, in_specs=in_specs, out_specs=P(AXES, None), check_vma=False
    )
```

```python
import functools

import jax
import jax.numpy as jnp
from jax import lax
from jax.experimental import pallas as pl
from jax.experimental.pallas import tpu as pltpu
from jax.sharding import PartitionSpec as P

AXES = ("req", "kvh")
BLOCK = 80
COLS = 4
FOLD = 4


def dot32(a, b):
    return jnp.dot(a, b, preferred_element_type=jnp.float32)


def stay(x):
    return pltpu.with_memory_space_constraint(x, pltpu.HBM)


def dot_t(a, b):
    return lax.dot_general(a, b, (((1,), (1,)), ((), ())), preferred_element_type=jnp.float32)


def flags(mask):
    return mask.astype(jnp.float32).astype(jnp.bfloat16)


def iota(shape, axis):
    return lax.broadcasted_iota(jnp.int32, shape, axis)


def plan(routes, gates, send_ref, mix_ref):
    picks, tokens = routes.shape
    rows, lanes = send_ref.shape
    experts = rows // (2 * FOLD)
    same = flags(iota((tokens, tokens), 0) == iota((tokens, tokens), 1))
    high = gates.astype(jnp.bfloat16)
    low = (gates - high.astype(jnp.float32)).astype(jnp.bfloat16)
    named = dot_t(same, routes.astype(jnp.float32).astype(jnp.bfloat16))
    highs, lows = dot_t(same, high), dot_t(same, low)
    expert = iota((tokens, experts), 1).astype(jnp.float32)
    has = jnp.zeros((tokens, experts), jnp.float32)
    mix_high, mix_low = has, has
    for k in range(picks):
        match = named[:, k:k + 1] == expert
        has = jnp.where(match, 1.0, has)
        mix_high = jnp.where(match, highs[:, k:k + 1], mix_high)
        mix_low = jnp.where(match, lows[:, k:k + 1], mix_low)
    before = flags(iota((tokens, tokens), 1) < iota((tokens, tokens), 0))
    count = dot32(before, has.astype(jnp.bfloat16))

    pieces = 4
    span, step = experts // pieces, rows // pieces
    row, col = iota((step, 2 * span), 0), iota((step, 2 * span), 1)
    place = flags(((row & 1) * span + (row >> 3)) == col)
    keep = ((iota((step, lanes), 0) >> 1) & (FOLD - 1)) == iota((step, lanes), 1) // tokens
    row, col = iota((2 * span, step), 0), iota((2 * span, step), 1)
    place_t = flags(((col & 1) * span + (col >> 3)) == row)
    keep_t = ((iota((2 * lanes, step), 1) >> 1) & (FOLD - 1)) == (iota((2 * lanes, step), 0) & (lanes - 1)) // tokens

    def by_slot(values, n):
        part = slice(n * span, (n + 1) * span)
        return jnp.concatenate(
            [jnp.where(count == float(c), values, 0.0)[:, part] for c in range(2)], axis=1
        ).astype(jnp.bfloat16)

    for n in range(pieces):
        out = slice(n * step, (n + 1) * step)
        sends = dot_t(place, jnp.concatenate([by_slot(has, n)] * FOLD, axis=0))
        send_ref[out, :] = jnp.where(keep, sends, 0.0).astype(jnp.bfloat16)
        mixes = jnp.concatenate([by_slot(mix_high, n)] * FOLD + [by_slot(mix_low, n)] * FOLD, axis=0)
        mix_ref[:, out] = jnp.where(keep_t, dot32(mixes, place_t), 0.0).astype(jnp.bfloat16)


def attend_kernel(
    len_hbm, table_hbm, q_hbm, k_hbm, v_hbm, w_hbm, routes_hbm, logits_hbm, res_hbm, gain_hbm,
    out_ref, send_ref, mix_ref, res_ref, gain_ref,
    len_ref, table_ref, q_ref, k_buf, v_buf, w_buf, routes_ref, logits_ref,
    apart_ref, left_ref, s_ref, m_ref, o_ref, att_ref,
    in_sem, k_sem, v_sem, w_sem,
):
    pages, slots, dim = k_buf.shape
    requests, groups, _ = q_ref.shape
    columns = table_ref.shape[0]
    blocks = pages // BLOCK
    cols = out_ref.shape[1] // COLS

    def fetch(n, src, dst):
        return pltpu.make_async_copy(src, dst, in_sem.at[n])

    small = [
        fetch(0, len_hbm, len_ref), fetch(1, table_hbm, table_ref), fetch(2, q_hbm, q_ref),
        fetch(3, routes_hbm, routes_ref), fetch(4, logits_hbm, logits_ref),
        fetch(5, res_hbm, res_ref), fetch(6, gain_hbm, gain_ref),
    ]
    k_copies, v_copies = [], []
    for b in range(blocks):
        span = pl.ds(b * BLOCK, BLOCK)
        k_copies.append(pltpu.make_async_copy(k_hbm.at[span], k_buf.at[span], k_sem.at[b]))
        v_copies.append(pltpu.make_async_copy(v_hbm.at[span], v_buf.at[span], v_sem.at[b]))
    w_copies = []
    for c in range(COLS):
        span = slice(c * cols, (c + 1) * cols)
        w_copies.append(pltpu.make_async_copy(w_hbm.at[:, span], w_buf.at[:, span], w_sem.at[c]))
    for copy in small[:3] + k_copies + small[3:]:
        copy.start()

    small[0].wait()
    small[1].wait()
    lengths = len_ref[...]
    column = iota((columns, requests), 0)
    table = jnp.where(column < ((lengths + (slots - 1)) >> (slots.bit_length() - 1)), table_ref[...], -1)
    usable = lengths - column * slots
    half = columns // 2
    table = jnp.concatenate([table[:half], table[half:]], axis=1)
    usable = jnp.concatenate([usable[:half], usable[half:]], axis=1)
    page = iota((pages, 2 * requests), 0)
    left = jnp.zeros((pages, 2 * requests), jnp.int32)
    for c in range(half):
        left = jnp.where(table[c:c + 1, :] == page, usable[c:c + 1, :], left)
    left = left.astype(jnp.float32)
    owned = jnp.maximum(left[:, :requests], left[:, requests:]) > 0
    left_ref[:pages, :] = jnp.broadcast_to(jnp.max(left, axis=-1, keepdims=True), (pages, slots))
    apart_ref[...] = jnp.where(owned, 0.0, -jnp.inf)
    owned = flags(owned)
    same = flags(iota((requests, requests), 0) == iota((requests, requests), 1))
    pick = dot_t(same, owned).astype(jnp.bfloat16)

    def pair_rows(p):
        return pl.ds(p * groups, 2 * groups)

    def apart_rows(x):
        top = iota(x.shape, 0) < groups
        return jnp.concatenate([jnp.where(top, x, 0.0), jnp.where(top, 0.0, x)], axis=1).astype(jnp.bfloat16)

    def group_rows(g, count):
        return pl.ds(g, count, stride=groups)

    small[2].wait()
    o_ref[:requests * groups, :] = q_ref[...].reshape(requests * groups, dim).astype(jnp.float32)
    for g in range(groups):
        s_ref[group_rows(g, pages), :] = dot32(owned, o_ref[group_rows(g, requests), :].astype(jnp.bfloat16))

    lane = iota((2 * groups, slots), 1).astype(jnp.float32)
    for b in range(blocks):
        k_copies[b].wait()
        if b == 0:
            for copy in v_copies:
                copy.start()
        if b == blocks - 1:
            for copy in w_copies:
                copy.start()

        for p in range(b * BLOCK, (b + 1) * BLOCK, 2):
            keys = jnp.concatenate([k_buf[p], k_buf[p + 1]], axis=1)
            s = dot_t(apart_rows(s_ref[pair_rows(p), :]), keys) * dim ** (-0.5)
            limit = jnp.concatenate(
                [left_ref[pl.ds(p + i, groups, stride=0), :] for i in range(2)], axis=0
            )
            s = jnp.where(lane < limit, s, -jnp.inf)
            s_ref[pair_rows(p), :] = s
            m_ref[pair_rows(p), :] = jnp.broadcast_to(jnp.max(s, axis=-1, keepdims=True), s.shape)

    apart = apart_ref[...]
    for g in range(groups):
        peak = jnp.max(m_ref[group_rows(g, pages), :][:, :requests] + apart, axis=0, keepdims=True)
        peak = jnp.maximum(jnp.max(peak + apart, axis=-1, keepdims=True), -3e38)
        m_ref[group_rows(g, pages), :] = jnp.broadcast_to(peak, (pages, dim))

    for copy in small[3:]:
        copy.wait()
    logits = logits_ref[...]
    raised = jnp.exp(logits - jnp.max(logits, axis=0, keepdims=True))
    plan(
        routes_ref[...], raised / jnp.sum(raised, axis=0, keepdims=True), send_ref, mix_ref
    )

    for b in range(blocks):
        v_copies[b].wait()

        for p in range(b * BLOCK, (b + 1) * BLOCK, 2):
            w = jnp.exp(s_ref[pair_rows(p), :] - m_ref[pair_rows(p), :])
            m_ref[pair_rows(p), :] = jnp.broadcast_to(jnp.sum(w, axis=-1, keepdims=True), w.shape)
            values = jnp.concatenate([v_buf[p], v_buf[p + 1]], axis=0)
            o_ref[pair_rows(p), :] = dot32(apart_rows(w), values)

    def parts(values):
        high = values.astype(jnp.bfloat16).astype(jnp.float32)
        return high, values - high

    first = iota((pages, dim), 1) < dim // 2
    for g in range(groups):
        high, low = parts(o_ref[group_rows(g, pages), :])
        sums = jnp.where(first, *parts(m_ref[group_rows(g, pages), :]))
        total = dot32(pick, jnp.concatenate([high, low, sums], axis=1).astype(jnp.bfloat16))
        weight = total[:, 2 * dim:]
        weight = weight + pltpu.roll(weight, dim // 2, 1)
        att_ref[:, g * dim:(g + 1) * dim] = (
            (total[:, :dim] + total[:, dim:2 * dim]) / weight
        ).astype(jnp.bfloat16)

    att = att_ref[...]
    for c in range(COLS):
        span = slice(c * cols, (c + 1) * cols)
        w_copies[c].wait()
        out_ref[:, span] = dot32(att, w_buf[:, span]).astype(out_ref.dtype)


def attend(lengths, page_table, queries, key_cache, value_cache, w_out, routes, logits, residual, gain, experts):
    pages, slots, dim = key_cache.shape
    requests, groups, _ = queries.shape
    tokens = residual.shape[0]
    blocks = pages // BLOCK
    hbm = pl.BlockSpec(memory_space=pltpu.HBM)
    vmem = pl.BlockSpec(memory_space=pltpu.VMEM)
    rows, lanes = experts * 2 * FOLD, FOLD * tokens
    tile = pltpu.VMEM((pages * groups, dim), jnp.float32)
    args = (lengths, page_table, queries, key_cache, value_cache, w_out, routes, logits, residual, gain)
    return pl.pallas_call(
        attend_kernel,
        out_shape=(
            jax.ShapeDtypeStruct((requests, w_out.shape[1]), jnp.bfloat16),
            jax.ShapeDtypeStruct((rows, lanes), jnp.bfloat16),
            jax.ShapeDtypeStruct((2 * lanes, rows), jnp.bfloat16),
            jax.ShapeDtypeStruct(residual.shape, residual.dtype),
            jax.ShapeDtypeStruct(gain.shape, gain.dtype),
        ),
        in_specs=[hbm] * len(args),
        out_specs=(vmem,) * 5,
        scratch_shapes=[
            pltpu.VMEM(lengths.shape, jnp.int32),
            pltpu.VMEM(page_table.shape, jnp.int32),
            pltpu.VMEM(queries.shape, queries.dtype),
            pltpu.VMEM(key_cache.shape, key_cache.dtype),
            pltpu.VMEM(value_cache.shape, value_cache.dtype),
            pltpu.VMEM(w_out.shape, w_out.dtype),
            pltpu.VMEM(routes.shape, jnp.int32),
            pltpu.VMEM(logits.shape, jnp.float32),
            pltpu.VMEM((pages, requests), jnp.float32),
            pltpu.VMEM((pages + groups, slots), jnp.float32),
            tile, tile, tile,
            pltpu.VMEM((requests, groups * dim), jnp.bfloat16),
            pltpu.SemaphoreType.DMA((7,)),
            pltpu.SemaphoreType.DMA((blocks,)),
            pltpu.SemaphoreType.DMA((blocks,)),
            pltpu.SemaphoreType.DMA((COLS,)),
        ],
        compiler_params=pltpu.CompilerParams(vmem_limit_bytes=24 << 20),
        name="attend",
    )(*map(stay, args))


def dispatch_kernel(part_ref, res_ref, gain_ref, send_ref, stream_ref, out_ref):
    width = res_ref.shape[1]
    part = width // FOLD
    total = part_ref[0].astype(jnp.float32)
    for i in range(1, part_ref.shape[0]):
        total = total + part_ref[i].astype(jnp.float32)
    stream = res_ref[...].astype(jnp.float32) + total
    stream_ref[...] = stream
    inverse = lax.rsqrt(jnp.mean(stream * stream, axis=-1, keepdims=True) + 1e-06)
    gain = gain_ref[...].astype(jnp.float32)
    gain = jnp.concatenate([gain[i:i + 1] for i in range(gain.shape[0])], axis=1)
    normed = (stream * inverse * gain).astype(jnp.bfloat16)
    rows = jnp.concatenate([normed[:, f * part:(f + 1) * part] for f in range(FOLD)], axis=0)
    out_ref[...] = dot32(send_ref[...], rows).astype(out_ref.dtype)


def dispatch(parts, residual, gain, send):
    tokens, width = residual.shape
    vmem = pl.BlockSpec(memory_space=pltpu.VMEM)
    return pl.pallas_call(
        dispatch_kernel,
        out_shape=(
            jax.ShapeDtypeStruct((tokens, width), jnp.float32),
            jax.ShapeDtypeStruct((send.shape[0], width // FOLD), jnp.bfloat16),
        ),
        in_specs=[vmem] * 4,
        out_specs=(vmem, vmem),
        compiler_params=pltpu.CompilerParams(vmem_limit_bytes=8 << 20),
        name="dispatch",
    )(parts, residual, gain, send)


def expert_kernel(x_ref, gate_ref, up_ref, down_ref, out_ref, x_buf):
    rows, part = x_ref.shape
    group = 128
    inner = group // FOLD
    j, i = iota((group, group), 0), iota((group, group), 1)

    def source(row):
        return ((row & (inner - 1)) >> 1) * (2 * FOLD) + (row // inner) * 2 + (row & 1)

    unfold = (i == source(j)).astype(jnp.float32).astype(jnp.bfloat16)
    refold = (j == source(i)).astype(jnp.float32).astype(jnp.bfloat16)
    for n in range(rows // group):
        piece = dot32(unfold, x_ref[n * group:(n + 1) * group, :]).astype(jnp.bfloat16)
        for f in range(FOLD):
            x_buf[n * inner:(n + 1) * inner, f * part:(f + 1) * part] = piece[f * inner:(f + 1) * inner]
    x = x_buf[...]
    gate = dot32(x, gate_ref[...])
    up = dot32(x, up_ref[...])
    hidden = (gate / (1.0 + jnp.exp(-gate)) * up).astype(jnp.bfloat16)
    made = dot32(hidden, down_ref[...]).astype(jnp.bfloat16)
    for n in range(rows // group):
        piece = jnp.concatenate(
            [made[n * inner:(n + 1) * inner, f * part:(f + 1) * part] for f in range(FOLD)], axis=0
        )
        out_ref[n * group:(n + 1) * group, :] = dot32(refold, piece).astype(out_ref.dtype)


def expert(arrived, w_gate, w_up, w_down):
    vmem = pl.BlockSpec(memory_space=pltpu.VMEM)
    hbm = pl.BlockSpec(memory_space=pltpu.HBM)
    rows, part = arrived.shape
    return pl.pallas_call(
        expert_kernel,
        out_shape=jax.ShapeDtypeStruct(arrived.shape, jnp.bfloat16),
        in_specs=[vmem] * 4,
        out_specs=vmem,
        scratch_shapes=[
            pltpu.VMEM((rows // FOLD, part * FOLD), jnp.bfloat16),
        ],
        compiler_params=pltpu.CompilerParams(vmem_limit_bytes=16 << 20),
        name="expert",
    )(arrived, w_gate, w_up, w_down)


def combine_kernel(back_ref, stream_ref, mix_ref, out_ref):
    tokens = stream_ref.shape[0]
    part = back_ref.shape[1]
    total = dot32(mix_ref[...], back_ref[...])
    total = total[:FOLD * tokens] + total[FOLD * tokens:]
    for f in range(FOLD):
        span = slice(f * part, (f + 1) * part)
        out_ref[:, span] = (stream_ref[:, span] + total[f * tokens:(f + 1) * tokens]).astype(out_ref.dtype)


def combine(back, stream, mix):
    vmem = pl.BlockSpec(memory_space=pltpu.VMEM)
    return pl.pallas_call(
        combine_kernel,
        out_shape=jax.ShapeDtypeStruct(stream.shape, jnp.bfloat16),
        in_specs=[vmem] * 3,
        out_specs=vmem,
        compiler_params=pltpu.CompilerParams(vmem_limit_bytes=8 << 20),
        name="combine",
    )(back, stream, mix)


def local(
    queries,
    key_cache,
    value_cache,
    lengths,
    page_table,
    residual_in,
    w_out,
    norm_gain,
    route_logits,
    routes,
    w_gate,
    w_up,
    w_down,
):
    heads = lax.axis_size("kvh")
    experts = lax.axis_size("req") * heads
    tokens, width = residual_in.shape
    partial, send, mix, residual, gain = attend(
        lengths[None, :], page_table.T, queries[:, 0], key_cache[:, 0], value_cache[:, 0], w_out,
        routes.T, route_logits.T, residual_in, norm_gain.reshape(-1, 128), experts,
    )
    parts = lax.all_to_all(
        partial.reshape(heads, tokens, width), "kvh", split_axis=0, concat_axis=0, tiled=True
    )
    stream, outgoing = dispatch(parts, residual, gain, send)
    layout = (experts, 2 * FOLD, width // FOLD)
    exchange = functools.partial(lax.all_to_all, axis_name=AXES, split_axis=0, concat_axis=0, tiled=True)
    arrived = exchange(outgoing.reshape(layout)).reshape(outgoing.shape)
    produced = expert(arrived, w_gate[0], w_up[0], w_down[0])
    back = exchange(produced.reshape(layout)).reshape(outgoing.shape)
    return combine(back, stream, mix)


def solution(mesh):
    in_specs = (
        P("req", "kvh", None, None),
        P("req", "kvh", None, None),
        P("req", "kvh", None, None),
        P("req"),
        P("req", None),
        P(AXES, None),
        P("kvh", None),
        P(),
        P(AXES, None),
        P(AXES, None),
        P(AXES, None, None),
        P(AXES, None, None),
        P(AXES, None, None),
    )
    return jax.shard_map(
        local, mesh=mesh, in_specs=in_specs, out_specs=P(AXES, None), check_vma=False
    )
```
